256 devices in a mesh: ty: 16 (over x_hi, y, core), tx: 16 (over z, x_lo).
Axes of the slice: x: 4 (x_hi: 2, x_lo: 2; x = x_hi * 2 + x_lo), y: 4, z: 8, core: 2. Of those that a mesh axis runs over, the one named last changes fastest.
Arguments:
- object_slices: float32 [2, 2, 2048, 2048], P(None, None, 'ty', 'tx'), may hold values from -5 to 5
- probe: float32 [4, 2, 128, 128], replicated, may hold values from -4 to 4
- measured: float32 [16, 16, 4, 128, 128], P('ty', 'tx'), may hold values from 0 to 2
- offsets: int32 [2, 16, 16, 4], P(None, 'ty', 'tx'), may hold values from 0 to 127, as said below
- counts: int32 [16, 16], P('ty', 'tx'), may hold values from 1 to 4, as said below
Outputs:
- object_grad: float32 [2, 2, 2048, 2048], P(None, None, 'ty', 'tx')
- probe_grad: float32 [4, 2, 128, 128], replicated
The draws below stay inside these ranges and needn't reach their ends.
Inputs may be any that keep to these rules, and one draw needn't show every extreme that they name: `counts`: each tile has 1 to 4 live slots, and some tile has all 4 live. Every window lies inside the object: in the last tile row (column) the row (column) offset is at most 0. Slot 0 of every tile sits at the largest row and column offsets that its tile allows.
All inputs are finite; a program needn't handle non-finite values.
Results may differ from the reference program's by a relative error of at most 0.0003.
Values sent between devices are 32-bit elements; how exact they have to be, the bound alone decides.
A program may use at most 64 MiB of HBM per device.

```python
import math
import jax
import jax.numpy as jnp
from jax import lax

WINDOW = 128
MODES = 4
SLICES = 2
TILE = 128
CAP = 4
TILES_Y = 16
TILES_X = 16
NY = 2048
NX = 2048


def draw_counts(key, part):
    base_key, pick_key = jax.random.split(jax.random.fold_in(key, 11))
    total = TILES_Y * TILES_X
    base = jax.random.randint(base_key, (total,), 1, CAP + 1)
    chosen = jax.random.randint(pick_key, (), 0, total)
    filled = jnp.where(jnp.arange(total) == chosen, CAP, base)
    return filled.reshape(TILES_Y, TILES_X).astype(jnp.int32)


def draw_offsets(key, part):
    row_key, col_key = jax.random.split(jax.random.fold_in(key, 23))
    row_ids = jnp.arange(TILES_Y)[:, None, None]
    col_ids = jnp.arange(TILES_X)[None, :, None]
    row_high = jnp.where(row_ids == TILES_Y - 1, TILE - WINDOW, TILE - 1) + jnp.zeros((TILES_Y, TILES_X, CAP), jnp.int32)
    col_high = jnp.where(col_ids == TILES_X - 1, TILE - WINDOW, TILE - 1) + jnp.zeros((TILES_Y, TILES_X, CAP), jnp.int32)
    rows = jax.random.randint(row_key, (TILES_Y, TILES_X, CAP), 0, row_high + 1)
    cols = jax.random.randint(col_key, (TILES_Y, TILES_X, CAP), 0, col_high + 1)
    first = jnp.arange(CAP)[None, None, :] == 0
    rows = jnp.where(first, row_high, rows)
    cols = jnp.where(first, col_high, cols)
    return jnp.stack([rows, cols]).astype(jnp.int32)


def block_scale(own_key, dims, cuts, smallest, top_value):
    factor_of = 1.0
    for dim, shards_of in cuts:
        draws = jax.random.uniform(jax.random.fold_in(jax.random.fold_in(own_key, 6), dim), (shards_of,), jnp.float32, smallest / len(cuts), top_value / len(cuts))
        factor_of = factor_of * jnp.repeat(jnp.exp(draws), dims[dim] // shards_of).reshape((-1,) + (1,) * (len(dims) - 1 - dim))
    return factor_of


def gaussian(key, shape, deviation, limit, pieces=(), kind=jnp.bfloat16):
    entries = deviation * jax.random.normal(key, shape, jnp.float32)
    if pieces:
        entries = entries * block_scale(key, shape, pieces, -0.22, 0.18)
    return jnp.clip(entries, -limit, limit).astype(kind)


def setup_inputs(seed: int = 0) -> dict:
    arg_keys = jax.random.split(jax.random.key(seed), 6)
    object_slices = gaussian(arg_keys[0], (SLICES, 2, NY, NX), 0.7, 5.0, ((2, 16), (3, 16)), jnp.float32)
    probe = gaussian(arg_keys[1], (MODES, 2, WINDOW, WINDOW), 0.5, 4.0, (), jnp.float32)
    measured = jnp.clip(2.0 * jax.random.uniform(arg_keys[2], (TILES_Y, TILES_X, CAP, WINDOW, WINDOW), jnp.float32) ** block_scale(arg_keys[2], (TILES_Y, TILES_X, CAP, WINDOW, WINDOW), ((0, 16), (1, 16)), -0.2, 0.2), 0.0, 2.0)
    offsets = draw_offsets(jax.random.fold_in(arg_keys[5], 71), 0)
    counts = draw_counts(jax.random.fold_in(arg_keys[5], 71), 0)
    return dict(object_slices=object_slices, probe=probe, measured=measured, offsets=offsets, counts=counts)


def propagator_table():
    positions = jnp.arange(WINDOW, dtype=jnp.int32)
    freq = (positions + WINDOW // 2) % WINDOW - WINDOW // 2
    quad = (freq[:, None] * freq[:, None] + freq[None, :] * freq[None, :]) % (4 * WINDOW)
    angle = quad.astype(jnp.float32) * (-2.0 * math.pi / (4 * WINDOW))
    return lax.complex(jnp.cos(angle), jnp.sin(angle))

def tile_loss(windows, probe, measured_tile, live):
    propagator = propagator_table()
    probe_c = lax.complex(probe[:, 0], probe[:, 1])
    window_c = lax.complex(windows[:, :, 0], windows[:, :, 1])
    wave = probe_c[None] * window_c[:, 0][:, None]
    for layer in range(1, SLICES):
        spectrum = jnp.fft.fft2(wave, norm='ortho') * propagator
        wave = jnp.fft.ifft2(spectrum, norm='ortho') * window_c[:, layer][:, None]
    far_field = jnp.fft.fft2(wave, norm='ortho')
    intensity = lax.optimization_barrier(jnp.sum(jnp.real(far_field) ** 2 + jnp.imag(far_field) ** 2, axis=1))
    diff = (intensity - measured_tile) * live[:, None, None]
    return 0.5 * jnp.sum(diff * diff)

def reference(object_slices, probe, measured, offsets, counts):
    zero = jnp.zeros((), jnp.int32)

    def one_tile(carry, tile_id):
        grad_object, grad_probe = carry
        tile_row = (tile_id // TILES_X).astype(jnp.int32)
        tile_col = (tile_id % TILES_X).astype(jnp.int32)
        local = lax.dynamic_slice(offsets, (zero, tile_row, tile_col, zero), (2, 1, 1, CAP)).reshape(2, CAP)
        rows_at = (tile_row * TILE + local[0]).astype(jnp.int32)
        cols_at = (tile_col * TILE + local[1]).astype(jnp.int32)

        def cut_window(row_at, col_at):
            return lax.dynamic_slice(object_slices, (zero, zero, row_at, col_at), (SLICES, 2, WINDOW, WINDOW))
        windows = jax.vmap(cut_window)(rows_at, cols_at)
        measured_tile = lax.dynamic_slice(measured, (tile_row, tile_col, zero, zero, zero), (1, 1, CAP, WINDOW, WINDOW)).reshape(CAP, WINDOW, WINDOW)
        count = lax.dynamic_slice(counts, (tile_row, tile_col), (1, 1)).reshape(())
        live = (jnp.arange(CAP, dtype=jnp.int32) < count).astype(jnp.float32)
        loss_value, pull = jax.vjp(lambda wins, prb: tile_loss(wins, prb, measured_tile, live), windows, probe)
        grad_windows, grad_probe_tile = pull(jnp.ones_like(loss_value))

        def add_slot(slot, total):
            start = (zero, zero, rows_at[slot], cols_at[slot])
            current = lax.dynamic_slice(total, start, (SLICES, 2, WINDOW, WINDOW))
            return lax.dynamic_update_slice(total, current + grad_windows[slot], start)
        grad_object = lax.fori_loop(0, CAP, add_slot, grad_object)
        return ((grad_object, grad_probe + grad_probe_tile), None)
    start_carry = (jnp.zeros_like(object_slices), jnp.zeros_like(probe))
    (object_grad, probe_grad), _ = lax.scan(one_tile, start_carry, jnp.arange(TILES_Y * TILES_X, dtype=jnp.int32))
    return (object_grad, probe_grad)
```

```python
import ml_dtypes
import numpy as np

import jax
import jax.numpy as jnp
from jax import lax
from jax.experimental import pallas as pl
from jax.experimental.pallas import tpu as pltpu
from jax.sharding import PartitionSpec as P

W = 128
MODES = 4
SLOTS = 4
F32 = jnp.float32
BF16 = jnp.bfloat16


def tables():
    k = np.arange(W)
    f1 = np.exp(-2j * np.pi * (np.outer(k, k) % W) / W) / np.sqrt(W)
    freq = (k + W // 2) % W - W // 2
    h = np.exp(-2j * np.pi * (freq * freq % (4 * W)) / (4 * W))
    a = (np.conj(f1) * h[None, :]) @ f1
    out = []
    for m in (a, f1):
        right = np.block([[m.real, m.imag], [-m.imag, m.real]])
        for t in (right, right.T):
            hi = t.astype(ml_dtypes.bfloat16)
            lo = (t - hi.astype(np.float64)).astype(ml_dtypes.bfloat16)
            out.append(np.stack([hi, lo]))
    return np.stack(out)


def split(x):
    hi = x.astype(BF16)
    return hi, (x - hi.astype(F32)).astype(BF16)


def dot(a, b):
    return jnp.dot(a, b, preferred_element_type=F32)


def right_mul(x, tab):
    xh, xl = split(x)
    return dot(xh, tab[0]) + (dot(xl, tab[0]) + dot(xh, tab[1]))


def left_mul(tab, y):
    yh, yl = split(y)
    return dot(tab[0], yh) + (dot(tab[0], yl) + dot(tab[1], yh))


def pair(u0, u1):
    top = jnp.concatenate([u0[:, :W], u1[:, :W]], 1)
    return jnp.concatenate([top, jnp.concatenate([u0[:, W:], u1[:, W:]], 1)], 0)


def both(fields, rtab, ltab):
    x = jnp.concatenate([jnp.concatenate([r, i], 1) for r, i in fields], 0)
    y = right_mul(x, rtab)
    out = []
    for p in range(2):
        z = left_mul(ltab, pair(y[2 * p * W : (2 * p + 1) * W], y[(2 * p + 1) * W : (2 * p + 2) * W]))
        out.append((z[:W, :W], z[W:, :W]))
        out.append((z[:W, W:], z[W:, W:]))
    return out


def cmul(a, b):
    return a[0] * b[0] - a[1] * b[1], a[0] * b[1] + a[1] * b[0]


def cmulc(a, b):
    return a[0] * b[0] + a[1] * b[1], a[0] * b[1] - a[1] * b[0]


def add(a, b):
    return a[0] + b[0], a[1] + b[1]


def kernel(
    off, cnt, obj, probe_hbm, meas_hbm, tab_hbm, gobj, gprobe,
    probe, meas, tab, ext0, ext1, win, tbuf, gt, gwin, pad, gext0, gext1, glow, gright,
    acc, rcore, ra, rb, zb, res, lsem, ssem, rsem,
):
    ty, tx = lax.axis_index("ty"), lax.axis_index("tx")
    core, y, xh = lax.rem(ty, 2), lax.rem(lax.div(ty, 2), 4), lax.div(ty, 8)
    z, x = lax.div(tx, 2), xh * 2 + lax.rem(tx, 2)

    def at(core, y, x, z):
        return {"ty": lax.div(x, 2) * 8 + y * 2 + core, "tx": z * 2 + lax.rem(x, 2)}

    ext, gext = (ext0, ext1), (gext0, gext1)
    local = []
    for src, dst in (
        (obj.at[0], ext0.at[:, 0, 0:W, :]),
        (obj.at[1], ext1.at[:, 0, 0:W, :]),
        (probe_hbm, probe),
        (tab_hbm, tab),
        (meas_hbm, meas),
    ):
        local.append(pltpu.make_async_copy(src, dst, lsem.at[len(local)]))
        local[-1].start()

    left, right = {"ty": ty, "tx": lax.rem(tx + 15, 16)}, {"ty": ty, "tx": lax.rem(tx + 1, 16)}
    upper, lower = {"ty": lax.rem(ty + 15, 16), "tx": tx}, {"ty": lax.rem(ty + 1, 16), "tx": tx}
    peers = [at(1 - core, y, x, z), left, right, upper, lower]
    peers += [at(core, lax.rem(y + k, 4), x, z) for k in range(1, 4)]
    peers += [at(core, y, lax.rem(x + k, 4), z) for k in range(1, 4)]
    peers += [at(core, y, x, lax.rem(z + k, 8)) for k in range(1, 8)]
    barrier = pltpu.get_barrier_semaphore()
    for peer in peers:
        pl.semaphore_signal(barrier, inc=1, device_id=peer, device_id_type=pl.DeviceIdType.MESH)
    pl.semaphore_wait(barrier, len(peers))

    sent = []

    def remote(src, dst, device):
        i = len(sent)
        copy = pltpu.make_async_remote_copy(
            src_ref=src, dst_ref=dst, send_sem=ssem.at[i], recv_sem=rsem.at[i],
            device_id=device, device_id_type=pl.DeviceIdType.MESH,
        )
        sent.append(copy)
        return copy

    from_right = [remote(obj.at[s], ext[s].at[:, 1, 0:W, :], left) for s in range(2)]
    from_lower = [remote(obj.at[s], ext[s].at[:, 0, W : 2 * W, :], upper) for s in range(2)]
    from_corner = [remote(ext[s].at[:, 1, 0:W, :], ext[s].at[:, 1, W : 2 * W, :], upper) for s in range(2)]
    for s in range(2):
        from_right[s].start()

        @pl.when(ty > 0)
        def _():
            from_lower[s].start()

    for s in range(2):
        from_right[s].wait_recv()

        @pl.when(ty > 0)
        def _():
            from_corner[s].start()

    lane = lax.broadcasted_iota(jnp.int32, (W, W), 1)

    def halo_wait(s):
        local[s].wait()

        @pl.when(ty < 15)
        def _():
            from_lower[s].wait_recv()
            from_corner[s].wait_recv()

    def cut(slot, s):
        oy, ox = off[0, slot], off[1, slot]
        shift = lax.rem(W - ox, W)
        parts = []
        for c in range(2):
            first = pltpu.roll(ext[s][c, 0, pl.ds(oy, W), :], shift, 1)
            second = pltpu.roll(ext[s][c, 1, pl.ds(oy, W), :], shift, 1)
            parts.append(jnp.where(lane < W - ox, first, second))
            win[s, slot, c] = parts[c]
        return tuple(parts)

    def scatter(s):
        zero = jnp.zeros((W, W), F32)
        for c in range(2):
            for slot in range(SLOTS):
                oy, ox = off[0, slot], off[1, slot]
                g = pltpu.roll(gwin[s, slot, c], ox, 1)
                for half, mask in ((0, lane >= ox), (1, lane < ox)):
                    pad[half, W : 2 * W, :] = jnp.where(mask, g, zero)
                for half in range(2):
                    v = pad[half, pl.ds(W - oy, 2 * W), :]
                    if slot == 0:
                        gext[s][c, half] = v
                    else:
                        gext[s][c, half] += v

    for part in (0, 2):
        pad[:, part * W : (part + 1) * W, :] = jnp.zeros((2, W, W), F32)
    local[2].wait()
    local[3].wait()
    local[4].wait()
    a_r, a_l, f_r, f_l = (tab.at[i] for i in range(4))

    halo_wait(0)

    def first_layer(slot, _):
        w0 = cut(slot, 0)
        ts = both([cmul((probe[m, 0], probe[m, 1]), w0) for m in range(MODES)], a_r, a_l)
        for m in range(MODES):
            tbuf[slot, m, 0], tbuf[slot, m, 1] = ts[m]
        return 0

    lax.fori_loop(0, SLOTS, first_layer, 0)
    halo_wait(1)

    def second_layer(slot, _):
        w1 = cut(slot, 1)
        far = both([cmul((tbuf[slot, m, 0], tbuf[slot, m, 1]), w1) for m in range(MODES)], f_r, f_l)
        intensity = sum(r * r + i * i for r, i in far)
        live = jnp.where(slot < cnt[0, 0], 2.0, 0.0)
        d = (intensity - meas[slot]) * live
        gw = both([(r * d, i * d) for r, i in far], f_l, f_r)
        total = None
        for m in range(MODES):
            gt[slot, m, 0], gt[slot, m, 1] = cmulc(w1, gw[m])
            g = cmulc((tbuf[slot, m, 0], tbuf[slot, m, 1]), gw[m])
            total = g if total is None else add(total, g)
        gwin[1, slot, 0], gwin[1, slot, 1] = total
        return 0

    lax.fori_loop(0, SLOTS, second_layer, 0)

    to_lower = [remote(gext[s].at[:, :, W : 2 * W, :], glow.at[s], lower) for s in range(2)]
    to_right = [remote(gext[s].at[:, 1, 0:W, :], gright.at[s], right) for s in range(2)]

    def send_down(s):
        scatter(s)

        @pl.when(ty < 15)
        def _():
            to_lower[s].start()

    def send_right(s):
        @pl.when(ty > 0)
        def _():
            to_lower[s].wait_recv()
            for c in range(2):
                for half in range(2):
                    gext[s][c, half, 0:W, :] += glow[s, c, half]

        to_right[s].start()

    def finish(s):
        to_right[s].wait_recv()
        for c in range(2):
            gobj[s, c] = gext[s][c, 0, 0:W, :] + gright[s, c]

    send_down(1)

    def span(start, size):
        return pl.ds(pl.multiple_of(start, size), size)

    def axes(m):
        on_y = [at(core, lax.rem(y + k, 4), x, z) for k in range(4)]
        on_x = [at(core, y, lax.rem(x + k, 4), z) for k in range(4)]
        return (y, x, on_y, on_x) if m < 2 else (x, y, on_x, on_y)

    other = at(1 - core, y, x, z)
    mine = core * W
    by_core, by_a, by_b, by_z, out_b, out_a, out_core = ([] for _ in range(7))
    for m in range(MODES):
        a, b, on_a, on_b = axes(m)
        place = mine + a * 32 + b * 8
        by_core.append(remote(acc.at[m, span((1 - core) * W, W), :], rcore.at[m], other))
        by_a.append([remote(acc.at[m, span(mine + lax.rem(a + k, 4) * 32, 32), :], ra.at[m, k - 1], on_a[k]) for k in range(1, 4)])
        by_b.append([remote(acc.at[m, span(mine + a * 32 + lax.rem(b + k, 4) * 8, 8), :], rb.at[m, k - 1], on_b[k]) for k in range(1, 4)])
        by_z.append([remote(zb.at[m, z], zb.at[m, z], at(core, y, x, lax.rem(z + k, 8))) for k in range(1, 8)])
        own = res.at[m, span(place, 8), :]
        out_b.append([remote(own, own, on_b[k]) for k in range(1, 4)])
        own = res.at[m, span(mine + a * 32, 32), :]
        out_a.append([remote(own, own, on_a[k]) for k in range(1, 4)])
        own = res.at[m, span(mine, W), :]
        out_core.append(remote(own, own, other))

    def start(copies):
        for copy in copies:
            copy.start()

    def arrive(copies):
        for copy in copies:
            copy.wait_recv()

    for m in range(MODES):
        p = (probe[m, 0], probe[m, 1])
        gu = both([(gt[s, m, 0], gt[s, m, 1]) for s in range(SLOTS)], a_l, a_r)
        total = None
        for s in range(SLOTS):
            g = cmulc(p, gu[s])
            for c in range(2):
                if m == 0:
                    gwin[0, s, c] = g[c]
                else:
                    gwin[0, s, c] += g[c]
            q = cmulc((win[0, s, 0], win[0, s, 1]), gu[s])
            total = q if total is None else add(total, q)
        acc[m, 0:W, :], acc[m, W : 2 * W, :] = total
        by_core[m].start()

    send_right(1)
    for m in range(MODES):
        by_core[m].wait_recv()
        acc[m, span(mine, W), :] += rcore[m]
        start(by_a[m])
    send_down(0)
    for m in range(MODES):
        a, _, _, _ = axes(m)
        arrive(by_a[m])
        acc[m, span(mine + a * 32, 32), :] += ra[m, 0] + ra[m, 1] + ra[m, 2]
        start(by_b[m])
    finish(1)
    for m in range(MODES):
        a, b, _, _ = axes(m)
        arrive(by_b[m])
        zb[m, z] = acc[m, span(mine + a * 32 + b * 8, 8), :] + (rb[m, 0] + rb[m, 1] + rb[m, 2])
        start(by_z[m])
    send_right(0)
    for m in range(MODES):
        a, b, _, _ = axes(m)
        arrive(by_z[m])
        total = zb[m, 0]
        for k in range(1, 8):
            total = total + zb[m, k]
        res[m, span(mine + a * 32 + b * 8, 8), :] = total
        start(out_b[m])
    for m in range(MODES):
        arrive(out_b[m])
        start(out_a[m])
    finish(0)
    for m in range(MODES):
        arrive(out_a[m])
        out_core[m].start()
    for m in range(MODES):
        out_core[m].wait_recv()
        gprobe[m, 0] = res[m, 0:W, :]
        gprobe[m, 1] = res[m, W : 2 * W, :]

    up, down = from_lower + from_corner, to_lower
    for copy in sent:
        if not any(copy is c for c in up + down):
            copy.wait_send()

    @pl.when(ty > 0)
    def _():
        for copy in up:
            copy.wait_send()

    @pl.when(ty < 15)
    def _():
        for copy in down:
            copy.wait_send()


COPIES = 10 + MODES * 21


def on_device(object_slices, probe, measured, offsets, counts):
    smem, vmem, hbm = (pl.BlockSpec(memory_space=s) for s in (pltpu.SMEM, pltpu.VMEM, pl.ANY))
    shapes = [
        (MODES, 2, W, W),
        (SLOTS, W, W),
        None,
        (2, 2, 2 * W, W),
        (2, 2, 2 * W, W),
        (2, SLOTS, 2, W, W),
        (SLOTS, MODES, 2, W, W),
        (SLOTS, MODES, 2, W, W),
        (2, SLOTS, 2, W, W),
        (2, 3 * W, W),
        (2, 2, 2 * W, W),
        (2, 2, 2 * W, W),
        (2, 2, 2, W, W),
        (2, 2, W, W),
        (MODES, 2 * W, W),
        (MODES, W, W),
        (MODES, 3, 32, W),
        (MODES, 3, 8, W),
        (MODES, 8, 8, W),
        (MODES, 2 * W, W),
    ]
    scratch = [pltpu.VMEM(s, F32) if s else pltpu.VMEM((4, 2, 2 * W, 2 * W), BF16) for s in shapes]
    scratch += [pltpu.SemaphoreType.DMA((5,)), pltpu.SemaphoreType.DMA((COPIES,)), pltpu.SemaphoreType.DMA((COPIES,))]
    return pl.pallas_call(
        kernel,
        out_shape=(jax.ShapeDtypeStruct((2, 2, W, W), F32), jax.ShapeDtypeStruct((MODES, 2, W, W), F32)),
        in_specs=[smem, smem, hbm, hbm, hbm, hbm],
        out_specs=(vmem, vmem),
        scratch_shapes=scratch,
        compiler_params=pltpu.CompilerParams(collective_id=0, has_side_effects=True),
    )(
        offsets.reshape(2, SLOTS), counts, object_slices, probe, measured.reshape(SLOTS, W, W), jnp.asarray(tables())
    )


def solution(mesh):
    in_specs = (
        P(None, None, "ty", "tx"),
        P(),
        P("ty", "tx", None, None, None),
        P(None, "ty", "tx", None),
        P("ty", "tx"),
    )
    out_specs = (P(None, None, "ty", "tx"), P())
    return jax.shard_map(
        on_device, mesh=mesh, in_specs=in_specs, out_specs=out_specs, check_vma=False
    )
```

```python
import ml_dtypes
import numpy as np

import jax
import jax.numpy as jnp
from jax import lax
from jax.experimental import pallas as pl
from jax.experimental.pallas import tpu as pltpu
from jax.sharding import PartitionSpec as P

W = 128
MODES = 4
SLOTS = 4
F32 = jnp.float32
BF16 = jnp.bfloat16


def tables():
    k = np.arange(W)
    f1 = np.exp(-2j * np.pi * (np.outer(k, k) % W) / W) / np.sqrt(W)
    freq = (k + W // 2) % W - W // 2
    h = np.exp(-2j * np.pi * (freq * freq % (4 * W)) / (4 * W))
    a = (np.conj(f1) * h[None, :]) @ f1
    out = []
    for m in (a, f1):
        right = np.block([[m.real, m.imag], [-m.imag, m.real]])
        for t in (right, right.T):
            hi = t.astype(ml_dtypes.bfloat16)
            lo = (t - hi.astype(np.float64)).astype(ml_dtypes.bfloat16)
            out.append(np.stack([hi, lo]))
    return np.stack(out)


def split(x):
    hi = x.astype(BF16)
    return hi, (x - hi.astype(F32)).astype(BF16)


def dot(a, b):
    return jnp.dot(a, b, preferred_element_type=F32)


def right_mul(x, tab):
    xh, xl = split(x)
    return dot(xh, tab[0]) + (dot(xl, tab[0]) + dot(xh, tab[1]))


def left_mul(tab, y):
    yh, yl = split(y)
    return dot(tab[0], yh) + (dot(tab[0], yl) + dot(tab[1], yh))


def pair(u0, u1):
    top = jnp.concatenate([u0[:, :W], u1[:, :W]], 1)
    return jnp.concatenate([top, jnp.concatenate([u0[:, W:], u1[:, W:]], 1)], 0)


def both(fields, rtab, ltab):
    x = jnp.concatenate([jnp.concatenate([r, i], 1) for r, i in fields], 0)
    y = right_mul(x, rtab)
    out = []
    for p in range(2):
        z = left_mul(ltab, pair(y[2 * p * W : (2 * p + 1) * W], y[(2 * p + 1) * W : (2 * p + 2) * W]))
        out.append((z[:W, :W], z[W:, :W]))
        out.append((z[:W, W:], z[W:, W:]))
    return out


def cmul(a, b):
    return a[0] * b[0] - a[1] * b[1], a[0] * b[1] + a[1] * b[0]


def cmulc(a, b):
    return a[0] * b[0] + a[1] * b[1], a[0] * b[1] - a[1] * b[0]


def add(a, b):
    return a[0] + b[0], a[1] + b[1]


def kernel(
    off, cnt, obj, probe_hbm, meas_hbm, tab_hbm, gobj, gprobe,
    probe, meas, tab, ext0, ext1, win, tbuf, gt, gwin, pad, gext0, gext1, glow, gright, gside, gfar,
    acc, rcore, rp, zb, res, lsem, ssem, rsem,
):
    ty, tx = lax.axis_index("ty"), lax.axis_index("tx")
    core, y, xh = lax.rem(ty, 2), lax.rem(lax.div(ty, 2), 4), lax.div(ty, 8)
    z, x = lax.div(tx, 2), xh * 2 + lax.rem(tx, 2)

    def at(core, y, x, z):
        return {"ty": lax.div(x, 2) * 8 + y * 2 + core, "tx": z * 2 + lax.rem(x, 2)}

    ext, gext = (ext0, ext1), (gext0, gext1)
    local = []
    for src, dst in (
        (obj.at[0], ext0.at[:, 0, 0:W, :]),
        (obj.at[1], ext1.at[:, 0, 0:W, :]),
        (probe_hbm, probe),
        (tab_hbm, tab),
        (meas_hbm, meas),
    ):
        local.append(pltpu.make_async_copy(src, dst, lsem.at[len(local)]))
        local[-1].start()

    left, right = {"ty": ty, "tx": lax.rem(tx + 15, 16)}, {"ty": ty, "tx": lax.rem(tx + 1, 16)}
    upper, lower = {"ty": lax.rem(ty + 15, 16), "tx": tx}, {"ty": lax.rem(ty + 1, 16), "tx": tx}
    peers = [at(1 - core, y, x, z), left, right, upper, lower]
    peers += [{"ty": lax.rem(ty + 15, 16), "tx": lax.rem(tx + 15, 16)}, {"ty": lax.rem(ty + 1, 16), "tx": lax.rem(tx + 1, 16)}]
    plane = [(j, i) for j in (2, 1, 3, 0) for i in (2, 1, 3, 0)][:-1]
    in_plane = [at(core, lax.rem(y + j, 4), lax.rem(x + i, 4), z) for j, i in plane]
    in_line = [at(core, y, x, lax.rem(z + k, 8)) for k in (4, 3, 5, 2, 6, 1, 7)]
    peers += in_plane + in_line
    barrier = pltpu.get_barrier_semaphore()
    for peer in peers:
        pl.semaphore_signal(barrier, inc=1, device_id=peer, device_id_type=pl.DeviceIdType.MESH)
    pl.semaphore_wait(barrier, len(peers))

    sent = []

    def remote(src, dst, device):
        i = len(sent)
        copy = pltpu.make_async_remote_copy(
            src_ref=src, dst_ref=dst, send_sem=ssem.at[i], recv_sem=rsem.at[i],
            device_id=device, device_id_type=pl.DeviceIdType.MESH,
        )
        sent.append(copy)
        return copy

    from_right, from_lower, from_corner, far_corner, far_lower, far_direct = ([] for _ in range(6))
    up_left = {"ty": lax.rem(ty + 15, 16), "tx": lax.rem(tx + 15, 16)}
    for s in range(2):
        from_right.append([remote(obj.at[s, c], ext[s].at[c, 1, 0:W, :], left) for c in range(2)])
        from_lower.append(remote(obj.at[s], ext[s].at[:, 0, W : 2 * W, :], upper))
        from_corner.append([remote(ext[s].at[c, 1, 0:W, :], ext[s].at[c, 1, W : 2 * W, :], upper) for c in range(2)])
        far_corner.append([remote(obj.at[s, c], ext[s].at[c, 1, W : 2 * W, :], up_left) for c in range(2)])
        far_lower.append(remote(ext[s].at[0, 1, W : 2 * W, :], ext[s].at[0, 0, W : 2 * W, :], right))
        far_direct.append(remote(obj.at[s, 1], ext[s].at[1, 0, W : 2 * W, :], upper))
    sends_up = jnp.logical_and(ty > 0, ty != 8)
    gets_up = jnp.logical_and(ty < 15, ty != 7)
    first = tx == 0
    sends_far, gets_far = jnp.logical_and(ty == 8, tx > 0), jnp.logical_and(ty == 7, tx < 15)
    sends_direct, gets_direct = jnp.logical_and(ty == 8, first), jnp.logical_and(ty == 7, first)
    gets_relayed = jnp.logical_and(ty == 7, tx > 0)

    def send_left(s):
        for copy in from_right[s]:
            copy.start()

    def send_up(s):
        @pl.when(jnp.logical_or(sends_up, sends_direct))
        def _():
            from_lower[s].start()

    def relay(s):
        @pl.when(gets_far)
        def _():
            far_corner[s][0].wait_recv()
            far_lower[s].start()

        for c in range(2):
            from_right[s][c].wait_recv()

            @pl.when(sends_up)
            def _():
                from_corner[s][c].start()

    def send_far_up(s):
        @pl.when(sends_far)
        def _():
            for copy in (*far_corner[s], far_direct[s]):
                copy.start()

    send_far_up(0)
    send_up(0)
    send_left(0)
    relay(0)
    send_far_up(1)
    send_left(1)

    lane = lax.broadcasted_iota(jnp.int32, (W, W), 1)

    def halo_wait(s):
        local[s].wait()

        @pl.when(jnp.logical_or(gets_up, gets_direct))
        def _():
            from_lower[s].wait_recv()

        @pl.when(gets_up)
        def _():
            for copy in from_corner[s]:
                copy.wait_recv()

        @pl.when(gets_relayed)
        def _():
            far_lower[s].wait_recv()
            far_direct[s].wait_recv()

        @pl.when(gets_far)
        def _():
            far_corner[s][1].wait_recv()

    def cut(slot, s):
        oy, ox = off[0, slot], off[1, slot]
        shift = lax.rem(W - ox, W)
        parts = []
        for c in range(2):
            first = pltpu.roll(ext[s][c, 0, pl.ds(oy, W), :], shift, 1)
            second = pltpu.roll(ext[s][c, 1, pl.ds(oy, W), :], shift, 1)
            parts.append(jnp.where(lane < W - ox, first, second))
            win[s, slot, c] = parts[c]
        return tuple(parts)

    def scatter(s):
        zero = jnp.zeros((W, W), F32)
        for c in range(2):
            for slot in range(SLOTS):
                oy, ox = off[0, slot], off[1, slot]
                g = pltpu.roll(gwin[s, slot, c], ox, 1)
                for half, mask in ((0, lane >= ox), (1, lane < ox)):
                    pad[half, W : 2 * W, :] = jnp.where(mask, g, zero)
                for half in range(2):
                    v = pad[half, pl.ds(W - oy, 2 * W), :]
                    if slot == 0:
                        gext[s][c, half] = v
                    else:
                        gext[s][c, half] += v

    for part in (0, 2):
        pad[:, part * W : (part + 1) * W, :] = jnp.zeros((2, W, W), F32)
    local[2].wait()
    local[3].wait()
    local[4].wait()
    a_r, a_l, f_r, f_l = (tab.at[i] for i in range(4))

    halo_wait(0)
    send_up(1)

    def first_layer(slot, _):
        w0 = cut(slot, 0)
        ts = both([cmul((probe[m, 0], probe[m, 1]), w0) for m in range(MODES)], a_r, a_l)
        for m in range(MODES):
            tbuf[slot, m, 0], tbuf[slot, m, 1] = ts[m]
        return 0

    lax.fori_loop(0, SLOTS // 2, first_layer, 0)
    relay(1)
    lax.fori_loop(SLOTS // 2, SLOTS, first_layer, 0)
    halo_wait(1)

    def second_layer(slot, _):
        w1 = cut(slot, 1)
        far = both([cmul((tbuf[slot, m, 0], tbuf[slot, m, 1]), w1) for m in range(MODES)], f_r, f_l)
        intensity = sum(r * r + i * i for r, i in far)
        live = jnp.where(slot < cnt[0, 0], 2.0, 0.0)
        d = (intensity - meas[slot]) * live
        gw = both([(r * d, i * d) for r, i in far], f_l, f_r)
        total = None
        for m in range(MODES):
            gt[slot, m, 0], gt[slot, m, 1] = cmulc(w1, gw[m])
            g = cmulc((tbuf[slot, m, 0], tbuf[slot, m, 1]), gw[m])
            total = g if total is None else add(total, g)
        gwin[1, slot, 0], gwin[1, slot, 1] = total
        return 0

    lax.fori_loop(0, SLOTS, second_layer, 0)

    to_lower = [remote(gext[s].at[:, :, W : 2 * W, :], glow.at[s], lower) for s in range(2)]
    to_right = [remote(gext[s].at[:, 1, 0:W, :], gright.at[s], right) for s in range(2)]
    side = [remote(gext[s].at[:, 1, W : 2 * W, :], gside.at[s], right) for s in range(2)]
    down_far = [remote(gext[s].at[:, 0, W : 2 * W, :], gfar.at[s], lower) for s in range(2)]

    def send_down(s):
        scatter(s)

        @pl.when(ty == 7)
        def _():
            side[s].start()

    def down(s):
        @pl.when(gets_up)
        def _():
            to_lower[s].start()

    def send_far(s):
        @pl.when(ty == 7)
        def _():
            side[s].wait_recv()
            for c in range(2):
                gext[s][c, 0, W : 2 * W, :] += gside[s, c]
            down_far[s].start()

    def send_right(s):
        @pl.when(sends_up)
        def _():
            to_lower[s].wait_recv()
            for c in range(2):
                for half in range(2):
                    gext[s][c, half, 0:W, :] += glow[s, c, half]

        to_right[s].start()

    def finish(s):
        @pl.when(ty == 8)
        def _():
            down_far[s].wait_recv()
            for c in range(2):
                gext[s][c, 0, 0:W, :] += gfar[s, c]

        to_right[s].wait_recv()
        for c in range(2):
            gobj[s, c] = gext[s][c, 0, 0:W, :] + gright[s, c]

    send_down(1)
    down(1)

    def span(start, size):
        return pl.ds(pl.multiple_of(start, size), size)

    other = at(1 - core, y, x, z)
    mine = core * W
    place = span(mine + (y * 4 + x) * 8, 8)
    by_core, by_plane = [], []
    for m in range(MODES):
        by_core.append(remote(acc.at[m, span((1 - core) * W, W), :], rcore.at[m], other))
        by_plane.append([
            remote(acc.at[m, span(mine + (lax.rem(y + j, 4) * 4 + lax.rem(x + i, 4)) * 8, 8), :], rp.at[m, k], in_plane[k])
            for k, (j, i) in enumerate(plane)
        ])
    by_line, out_plane, out_core = [], [], []
    for g in range(2):
        pair_of = pl.ds(2 * g, 2)
        by_line.append([remote(zb.at[g, z], zb.at[g, z], device) for device in in_line])
        own = res.at[pair_of, place, :]
        out_plane.append([remote(own, own, device) for device in in_plane])
        out_core.append([])
        for j in (0, 1, 3, 2):
            own = res.at[pair_of, span(mine + lax.rem(y + 4 - j, 4) * 32, 32), :]
            out_core[g].append((j, remote(own, own, other)))

    def start(copies):
        for copy in copies:
            copy.start()

    def arrive(copies):
        for copy in copies:
            copy.wait_recv()

    def scatter_core(m):
        by_core[m].wait_recv()
        acc[m, span(mine, W), :] += rcore[m]
        start(by_plane[m])

    for m in range(MODES):
        p = (probe[m, 0], probe[m, 1])
        gu = both([(gt[s, m, 0], gt[s, m, 1]) for s in range(SLOTS)], a_l, a_r)
        total = None
        for s in range(SLOTS):
            g = cmulc(p, gu[s])
            for c in range(2):
                if m == 0:
                    gwin[0, s, c] = g[c]
                else:
                    gwin[0, s, c] += g[c]
            q = cmulc((win[0, s, 0], win[0, s, 1]), gu[s])
            total = q if total is None else add(total, q)
        acc[m, 0:W, :], acc[m, W : 2 * W, :] = total
        by_core[m].start()
        if m > 0:
            scatter_core(m - 1)
        if m == MODES - 1:
            send_far(1)

    scatter_core(MODES - 1)
    send_down(0)
    down(0)
    send_right(1)
    for g in range(2):
        for i in range(2):
            m = 2 * g + i
            arrive(by_plane[m])
            total = acc[m, place, :]
            for k in range(15):
                total = total + rp[m, k]
            zb[g, z, i] = total
        start(by_line[g])
    send_far(0)
    send_right(0)
    for g in range(2):
        arrive(by_line[g])
        for i in range(2):
            total = zb[g, 0, i]
            for k in range(1, 8):
                total = total + zb[g, k, i]
            res[2 * g + i, place, :] = total
        start(out_plane[g])
    for g in range(2):
        for j, copy in out_core[g]:
            arrive([out_plane[g][k] for k in range(15) if plane[k][0] == j])
            copy.start()
    finish(1)
    finish(0)
    for g in range(2):
        for _, copy in out_core[g]:
            copy.wait_recv()
        for m in (2 * g, 2 * g + 1):
            gprobe[m, 0] = res[m, 0:W, :]
            gprobe[m, 1] = res[m, W : 2 * W, :]

    groups = (
        (jnp.logical_or(sends_up, sends_direct), from_lower),
        (sends_up, from_corner[0] + from_corner[1]),
        (sends_far, far_corner[0] + far_corner[1] + far_direct),
        (gets_far, far_lower),
        (gets_up, to_lower),
        (ty == 7, side + down_far),
    )
    some = [id(copy) for _, copies in groups for copy in copies]
    for copy in sent:
        if id(copy) not in some:
            copy.wait_send()
    for condition, copies in groups:

        @pl.when(condition)
        def _():
            for copy in copies:
                copy.wait_send()


COPIES = 26 + MODES * 16 + 2 * 26


def on_device(object_slices, probe, measured, offsets, counts):
    smem, vmem, hbm = (pl.BlockSpec(memory_space=s) for s in (pltpu.SMEM, pltpu.VMEM, pl.ANY))
    shapes = [
        (MODES, 2, W, W),
        (SLOTS, W, W),
        None,
        (2, 2, 2 * W, W),
        (2, 2, 2 * W, W),
        (2, SLOTS, 2, W, W),
        (SLOTS, MODES, 2, W, W),
        (SLOTS, MODES, 2, W, W),
        (2, SLOTS, 2, W, W),
        (2, 3 * W, W),
        (2, 2, 2 * W, W),
        (2, 2, 2 * W, W),
        (2, 2, 2, W, W),
        (2, 2, W, W),
        (2, 2, W, W),
        (2, 2, W, W),
        (MODES, 2 * W, W),
        (MODES, W, W),
        (MODES, 15, 8, W),
        (2, 8, 2, 8, W),
        (MODES, 2 * W, W),
    ]
    scratch = [pltpu.VMEM(s, F32) if s else pltpu.VMEM((4, 2, 2 * W, 2 * W), BF16) for s in shapes]
    scratch += [pltpu.SemaphoreType.DMA((5,)), pltpu.SemaphoreType.DMA((COPIES,)), pltpu.SemaphoreType.DMA((COPIES,))]
    return pl.pallas_call(
        kernel,
        out_shape=(jax.ShapeDtypeStruct((2, 2, W, W), F32), jax.ShapeDtypeStruct((MODES, 2, W, W), F32)),
        in_specs=[smem, smem, hbm, hbm, hbm, hbm],
        out_specs=(vmem, vmem),
        scratch_shapes=scratch,
        compiler_params=pltpu.CompilerParams(collective_id=0, has_side_effects=True),
    )(
        offsets.reshape(2, SLOTS), counts, object_slices, probe, measured.reshape(SLOTS, W, W), jnp.asarray(tables())
    )


def solution(mesh):
    in_specs = (
        P(None, None, "ty", "tx"),
        P(),
        P("ty", "tx", None, None, None),
        P(None, "ty", "tx", None),
        P("ty", "tx"),
    )
    out_specs = (P(None, None, "ty", "tx"), P())
    return jax.shard_map(
        on_device, mesh=mesh, in_specs=in_specs, out_specs=out_specs, check_vma=False
    )
```

```python
import ml_dtypes
import numpy as np

import jax
import jax.numpy as jnp
from jax import lax
from jax.experimental import pallas as pl
from jax.experimental.pallas import tpu as pltpu
from jax.sharding import PartitionSpec as P

W = 128
MODES = 4
SLOTS = 4
F32 = jnp.float32
BF16 = jnp.bfloat16


def tables():
    k = np.arange(W)
    f1 = np.exp(-2j * np.pi * (np.outer(k, k) % W) / W) / np.sqrt(W)
    freq = (k + W // 2) % W - W // 2
    h = np.exp(-2j * np.pi * (freq * freq % (4 * W)) / (4 * W))
    a = (np.conj(f1) * h[None, :]) @ f1
    out = []
    for m in (a, f1):
        right = np.block([[m.real, m.imag], [-m.imag, m.real]])
        for t in (right, right.T):
            hi = t.astype(ml_dtypes.bfloat16)
            lo = (t - hi.astype(np.float64)).astype(ml_dtypes.bfloat16)
            out.append(np.stack([hi, lo]))
    return np.stack(out)


def split(x):
    hi = x.astype(BF16)
    return hi, (x - hi.astype(F32)).astype(BF16)


def dot(a, b):
    return jnp.dot(a, b, preferred_element_type=F32)


def right_mul(x, tab):
    xh, xl = split(x)
    return dot(xh, tab[0]) + (dot(xl, tab[0]) + dot(xh, tab[1]))


def left_mul(tab, y):
    yh, yl = split(y)
    return dot(tab[0], yh) + (dot(tab[0], yl) + dot(tab[1], yh))


def pair(u0, u1):
    top = jnp.concatenate([u0[:, :W], u1[:, :W]], 1)
    return jnp.concatenate([top, jnp.concatenate([u0[:, W:], u1[:, W:]], 1)], 0)


def both(fields, rtab, ltab):
    out = []
    for p in range(0, len(fields), 2):
        x = jnp.concatenate([jnp.concatenate([r, i], 1) for r, i in fields[p : p + 2]], 0)
        y = right_mul(x, rtab)
        z = left_mul(ltab, pair(y[:W], y[W:]))
        out.append((z[:W, :W], z[W:, :W]))
        out.append((z[:W, W:], z[W:, W:]))
    return out


def cmul(a, b):
    return a[0] * b[0] - a[1] * b[1], a[0] * b[1] + a[1] * b[0]


def cmulc(a, b):
    return a[0] * b[0] + a[1] * b[1], a[0] * b[1] - a[1] * b[0]


def add(a, b):
    return a[0] + b[0], a[1] + b[1]


def kernel(
    off, cnt, obj, probe_hbm, meas_hbm, tab_hbm, gobj, gprobe,
    probe, meas, tab, ext0, ext1, win, tbuf, gt, gwin, pad, gext0, gext1, glow, gright, gside, gfar,
    acc, rcore, rp, zb, res, lsem, ssem, rsem,
):
    ty, tx = lax.axis_index("ty"), lax.axis_index("tx")
    core, y, xh = lax.rem(ty, 2), lax.rem(lax.div(ty, 2), 4), lax.div(ty, 8)
    z, x = lax.div(tx, 2), xh * 2 + lax.rem(tx, 2)

    def at(core, y, x, z):
        return {"ty": lax.div(x, 2) * 8 + y * 2 + core, "tx": z * 2 + lax.rem(x, 2)}

    ext, gext = (ext0, ext1), (gext0, gext1)
    local = []
    for src, dst in (
        (obj.at[0], ext0.at[:, 0, 0:W, :]),
        (obj.at[1], ext1.at[:, 0, 0:W, :]),
        (probe_hbm, probe),
        (tab_hbm, tab),
        (meas_hbm, meas),
    ):
        local.append(pltpu.make_async_copy(src, dst, lsem.at[len(local)]))
        local[-1].start()

    left, right = {"ty": ty, "tx": lax.rem(tx + 15, 16)}, {"ty": ty, "tx": lax.rem(tx + 1, 16)}
    upper, lower = {"ty": lax.rem(ty + 15, 16), "tx": tx}, {"ty": lax.rem(ty + 1, 16), "tx": tx}
    peers = [at(1 - core, y, x, z), left, right, upper, lower]
    peers += [{"ty": lax.rem(ty + 15, 16), "tx": lax.rem(tx + 15, 16)}, {"ty": lax.rem(ty + 1, 16), "tx": lax.rem(tx + 1, 16)}]
    plane = [(j, i) for j in (2, 1, 3, 0) for i in (2, 1, 3, 0)][:-1]
    in_plane = [at(core, lax.rem(y + j, 4), lax.rem(x + i, 4), z) for j, i in plane]
    in_line = [at(core, y, x, lax.rem(z + k, 8)) for k in (4, 3, 5, 2, 6, 1, 7)]
    peers += in_plane + in_line
    barrier = pltpu.get_barrier_semaphore()
    for peer in peers:
        pl.semaphore_signal(barrier, inc=1, device_id=peer, device_id_type=pl.DeviceIdType.MESH)
    pl.semaphore_wait(barrier, len(peers))

    sent = []

    def remote(src, dst, device):
        i = len(sent)
        copy = pltpu.make_async_remote_copy(
            src_ref=src, dst_ref=dst, send_sem=ssem.at[i], recv_sem=rsem.at[i],
            device_id=device, device_id_type=pl.DeviceIdType.MESH,
        )
        sent.append(copy)
        return copy

    from_right, from_lower, from_corner, far_corner = ([] for _ in range(4))
    up_left = {"ty": lax.rem(ty + 15, 16), "tx": lax.rem(tx + 15, 16)}
    for s in range(2):
        from_right.append([remote(obj.at[s, c], ext[s].at[c, 1, 0:W, :], left) for c in range(2)])
        from_lower.append(remote(obj.at[s], ext[s].at[:, 0, W : 2 * W, :], upper))
        from_corner.append([remote(ext[s].at[c, 1, 0:W, :], ext[s].at[c, 1, W : 2 * W, :], upper) for c in range(2)])
        far_corner.append([remote(obj.at[s, c], ext[s].at[c, 1, W : 2 * W, :], up_left) for c in range(2)])
    far_lower = remote(ext0.at[0, 1, W : 2 * W, :], ext0.at[0, 0, W : 2 * W, :], right)
    far_direct = remote(obj.at[0, 1], ext0.at[1, 0, W : 2 * W, :], upper)
    sends_up = jnp.logical_and(ty > 0, ty != 8)
    gets_up = jnp.logical_and(ty < 15, ty != 7)
    first = tx == 0
    sends_far, gets_far = jnp.logical_and(ty == 8, tx > 0), jnp.logical_and(ty == 7, tx < 15)
    sends_direct, gets_direct = jnp.logical_and(ty == 8, first), jnp.logical_and(ty == 7, first)
    gets_relayed = jnp.logical_and(ty == 7, tx > 0)

    def send_left(s):
        for copy in from_right[s]:
            copy.start()

    def send_up(s):
        @pl.when(jnp.logical_or(sends_up, sends_direct) if s == 0 else ty > 0)
        def _():
            from_lower[s].start()

    def relay(s):
        if s == 0:

            @pl.when(gets_far)
            def _():
                far_corner[0][0].wait_recv()
                far_lower.start()

        for c in range(2):
            from_right[s][c].wait_recv()

            @pl.when(sends_up)
            def _():
                from_corner[s][c].start()

    def send_far_up(s):
        @pl.when(sends_far)
        def _():
            for copy in (*far_corner[s], *([far_direct] if s == 0 else [])):
                copy.start()

    send_far_up(0)
    send_up(0)
    send_left(0)
    send_left(1)
    relay(0)
    send_far_up(1)
    send_up(1)

    lane = lax.broadcasted_iota(jnp.int32, (W, W), 1)

    def halo_wait(s):
        local[s].wait()

        @pl.when(jnp.logical_or(gets_up, gets_direct) if s == 0 else ty < 15)
        def _():
            from_lower[s].wait_recv()

        @pl.when(gets_up)
        def _():
            for copy in from_corner[s]:
                copy.wait_recv()

        @pl.when(gets_relayed)
        def _():
            if s == 0:
                far_lower.wait_recv()
                far_direct.wait_recv()

        @pl.when(gets_far)
        def _():
            for copy in far_corner[s][1 - s :]:
                copy.wait_recv()

    def cut(slot, s):
        oy, ox = off[0, slot], off[1, slot]
        shift = lax.rem(W - ox, W)
        parts = []
        for c in range(2):
            first = pltpu.roll(ext[s][c, 0, pl.ds(oy, W), :], shift, 1)
            second = pltpu.roll(ext[s][c, 1, pl.ds(oy, W), :], shift, 1)
            parts.append(jnp.where(lane < W - ox, first, second))
            win[s, slot, c] = parts[c]
        return tuple(parts)

    def scatter(s):
        zero = jnp.zeros((W, W), F32)
        for c in range(2):
            for slot in range(SLOTS):
                oy, ox = off[0, slot], off[1, slot]
                g = pltpu.roll(gwin[s, slot, c], ox, 1)
                for half, mask in ((0, lane >= ox), (1, lane < ox)):
                    pad[half, W : 2 * W, :] = jnp.where(mask, g, zero)
                for half in range(2):
                    v = pad[half, pl.ds(W - oy, 2 * W), :]
                    if slot == 0:
                        gext[s][c, half] = v
                    else:
                        gext[s][c, half] += v

    for part in (0, 2):
        pad[:, part * W : (part + 1) * W, :] = jnp.zeros((2, W, W), F32)
    local[2].wait()
    local[3].wait()
    local[4].wait()
    a_r, a_l, f_r, f_l = (tab.at[i] for i in range(4))

    halo_wait(0)

    def first_layer(slot):
        w0 = cut(slot, 0)
        ts = both([cmul((probe[m, 0], probe[m, 1]), w0) for m in range(MODES)], a_r, a_l)
        for m in range(MODES):
            tbuf[slot, m, 0], tbuf[slot, m, 1] = ts[m]

    for slot in range(0, SLOTS // 2):
        first_layer(slot)
    relay(1)
    for slot in range(SLOTS // 2, SLOTS):
        first_layer(slot)
    halo_wait(1)

    def second_layer(slot):
        w1 = cut(slot, 1)
        far = both([cmul((tbuf[slot, m, 0], tbuf[slot, m, 1]), w1) for m in range(MODES)], f_r, f_l)
        intensity = sum(r * r + i * i for r, i in far)
        live = jnp.where(slot < cnt[0, 0], 2.0, 0.0)
        d = (intensity - meas[slot]) * live
        gw = both([(r * d, i * d) for r, i in far], f_l, f_r)
        total = None
        for m in range(MODES):
            gt[slot, m, 0], gt[slot, m, 1] = cmulc(w1, gw[m])
            g = cmulc((tbuf[slot, m, 0], tbuf[slot, m, 1]), gw[m])
            total = g if total is None else add(total, g)
        gwin[1, slot, 0], gwin[1, slot, 1] = total

    for slot in range(SLOTS):
        second_layer(slot)

    to_lower = [remote(gext[s].at[:, :, W : 2 * W, :], glow.at[s], lower) for s in range(2)]
    to_right = [remote(gext[s].at[:, 1, 0:W, :], gright.at[s], right) for s in range(2)]
    side = [remote(gext[s].at[:, 1, W : 2 * W, :], gside.at[s], right) for s in range(2)]
    down_far = [remote(gext[s].at[:, 0, W : 2 * W, :], gfar.at[s], lower) for s in range(2)]

    def send_down(s):
        scatter(s)

        @pl.when(ty == 7)
        def _():
            side[s].start()

    def down(s):
        @pl.when(gets_up)
        def _():
            to_lower[s].start()

    def send_far(s):
        @pl.when(ty == 7)
        def _():
            side[s].wait_recv()
            for c in range(2):
                gext[s][c, 0, W : 2 * W, :] += gside[s, c]
            down_far[s].start()

    def send_right(s):
        @pl.when(sends_up)
        def _():
            to_lower[s].wait_recv()
            for c in range(2):
                for half in range(2):
                    gext[s][c, half, 0:W, :] += glow[s, c, half]

        to_right[s].start()

    def finish(s):
        @pl.when(ty == 8)
        def _():
            down_far[s].wait_recv()
            for c in range(2):
                gext[s][c, 0, 0:W, :] += gfar[s, c]

        to_right[s].wait_recv()
        for c in range(2):
            gobj[s, c] = gext[s][c, 0, 0:W, :] + gright[s, c]

    send_down(1)
    down(1)

    def span(start, size):
        return pl.ds(pl.multiple_of(start, size), size)

    other = at(1 - core, y, x, z)
    mine = core * W
    place = span(mine + (y * 4 + x) * 8, 8)
    by_core = [remote(acc.at[m, span((1 - core) * W, W), :], rcore.at[m], other) for m in range(MODES)]
    by_plane = []
    for g in range(2):
        spots = [span(mine + (lax.rem(y + j, 4) * 4 + lax.rem(x + i, 4)) * 8, 8) for j, i in plane]
        by_plane.append([remote(acc.at[pl.ds(2 * g, 2), spots[k], :], rp.at[g, k], in_plane[k]) for k in range(15)])
    by_line, out_plane, out_core = [], [], []
    for g in range(2):
        pair_of = pl.ds(2 * g, 2)
        by_line.append([remote(zb.at[g, z], zb.at[g, z], device) for device in in_line])
        own = res.at[pair_of, place, :]
        out_plane.append([remote(own, own, device) for device in in_plane])
        out_core.append([])
        for j in (0, 1, 3, 2):
            own = res.at[pair_of, span(mine + lax.rem(y + 4 - j, 4) * 32, 32), :]
            out_core[g].append((j, remote(own, own, other)))

    def start(copies):
        for copy in copies:
            copy.start()

    def arrive(copies):
        for copy in copies:
            copy.wait_recv()

    def scatter_core(g):
        for m in (2 * g, 2 * g + 1):
            by_core[m].wait_recv()
            acc[m, span(mine, W), :] += rcore[m]
        start(by_plane[g])

    for m in range(MODES):
        p = (probe[m, 0], probe[m, 1])
        gu = both([(gt[s, m, 0], gt[s, m, 1]) for s in range(SLOTS)], a_l, a_r)
        total = None
        for s in range(SLOTS):
            g = cmulc(p, gu[s])
            for c in range(2):
                if m == 0:
                    gwin[0, s, c] = g[c]
                else:
                    gwin[0, s, c] += g[c]
            q = cmulc((win[0, s, 0], win[0, s, 1]), gu[s])
            total = q if total is None else add(total, q)
        acc[m, 0:W, :], acc[m, W : 2 * W, :] = total
        if m % 2 == 0:
            continue
        start(by_core[m - 1 : m + 1])
        if m == MODES - 1:
            send_far(1)
            scatter_core(0)

    scatter_core(1)
    send_down(0)
    for g in range(2):
        for i in range(2):
            m = 2 * g + i
            if i == 0:
                arrive(by_plane[g])
            total = acc[m, place, :]
            for k in range(15):
                total = total + rp[g, k, i]
            zb[g, z, i] = total
        start(by_line[g])
    send_right(1)
    down(0)
    send_far(0)
    for g in range(2):
        arrive(by_line[g])
        for i in range(2):
            total = zb[g, 0, i]
            for k in range(1, 8):
                total = total + zb[g, k, i]
            res[2 * g + i, place, :] = total
        start(out_plane[g])
    send_right(0)
    for g in range(2):
        for j, copy in out_core[g]:
            arrive([out_plane[g][k] for k in range(15) if plane[k][0] == j])
            copy.start()
    finish(1)
    finish(0)
    for g in range(2):
        for _, copy in out_core[g]:
            copy.wait_recv()
        for m in (2 * g, 2 * g + 1):
            gprobe[m, 0] = res[m, 0:W, :]
            gprobe[m, 1] = res[m, W : 2 * W, :]

    groups = (
        (jnp.logical_or(sends_up, sends_direct), from_lower[:1]),
        (ty > 0, from_lower[1:]),
        (sends_up, from_corner[0] + from_corner[1]),
        (sends_far, far_corner[0] + far_corner[1] + [far_direct]),
        (gets_far, [far_lower]),
        (gets_up, to_lower),
        (ty == 7, side + down_far),
    )
    some = [id(copy) for _, copies in groups for copy in copies]
    for copy in sent:
        if id(copy) not in some:
            copy.wait_send()
    for condition, copies in groups:

        @pl.when(condition)
        def _():
            for copy in copies:
                copy.wait_send()


COPIES = 24 + MODES + 2 * 41


def on_device(object_slices, probe, measured, offsets, counts):
    smem, vmem, hbm = (pl.BlockSpec(memory_space=s) for s in (pltpu.SMEM, pltpu.VMEM, pl.ANY))
    shapes = [
        (MODES, 2, W, W),
        (SLOTS, W, W),
        None,
        (2, 2, 2 * W, W),
        (2, 2, 2 * W, W),
        (2, SLOTS, 2, W, W),
        (SLOTS, MODES, 2, W, W),
        (SLOTS, MODES, 2, W, W),
        (2, SLOTS, 2, W, W),
        (2, 3 * W, W),
        (2, 2, 2 * W, W),
        (2, 2, 2 * W, W),
        (2, 2, 2, W, W),
        (2, 2, W, W),
        (2, 2, W, W),
        (2, 2, W, W),
        (MODES, 2 * W, W),
        (MODES, W, W),
        (2, 15, 2, 8, W),
        (2, 8, 2, 8, W),
        (MODES, 2 * W, W),
    ]
    scratch = [pltpu.VMEM(s, F32) if s else pltpu.VMEM((4, 2, 2 * W, 2 * W), BF16) for s in shapes]
    scratch += [pltpu.SemaphoreType.DMA((5,)), pltpu.SemaphoreType.DMA((COPIES,)), pltpu.SemaphoreType.DMA((COPIES,))]
    return pl.pallas_call(
        kernel,
        out_shape=(jax.ShapeDtypeStruct((2, 2, W, W), F32), jax.ShapeDtypeStruct((MODES, 2, W, W), F32)),
        in_specs=[smem, smem, hbm, hbm, hbm, hbm],
        out_specs=(vmem, vmem),
        scratch_shapes=scratch,
        compiler_params=pltpu.CompilerParams(collective_id=0, has_side_effects=True),
    )(
        offsets.reshape(2, SLOTS), counts, object_slices, probe, measured.reshape(SLOTS, W, W), jnp.asarray(tables())
    )


def solution(mesh):
    in_specs = (
        P(None, None, "ty", "tx"),
        P(),
        P("ty", "tx", None, None, None),
        P(None, "ty", "tx", None),
        P("ty", "tx"),
    )
    out_specs = (P(None, None, "ty", "tx"), P())
    return jax.shard_map(
        on_device, mesh=mesh, in_specs=in_specs, out_specs=out_specs, check_vma=False
    )
```

```python
import ml_dtypes
import numpy as np

import jax
import jax.numpy as jnp
from jax import lax
from jax.experimental import pallas as pl
from jax.experimental.pallas import tpu as pltpu
from jax.sharding import PartitionSpec as P

W = 128
MODES = 4
SLOTS = 4
F32 = jnp.float32
BF16 = jnp.bfloat16


def tables():
    k = np.arange(W)
    f1 = np.exp(-2j * np.pi * (np.outer(k, k) % W) / W) / np.sqrt(W)
    freq = (k + W // 2) % W - W // 2
    h = np.exp(-2j * np.pi * (freq * freq % (4 * W)) / (4 * W))
    a = (np.conj(f1) * h[None, :]) @ f1
    out = []
    for m in (a, f1):
        right = np.block([[m.real, m.imag], [-m.imag, m.real]])
        for t in (right, right.T):
            hi = t.astype(ml_dtypes.bfloat16)
            lo = (t - hi.astype(np.float64)).astype(ml_dtypes.bfloat16)
            out.append(np.stack([hi, lo]))
    return np.stack(out)


def split(x):
    hi = x.astype(BF16)
    return hi, (x - hi.astype(F32)).astype(BF16)


def dot(a, b):
    return jnp.dot(a, b, preferred_element_type=F32)


def right_mul(x, tab):
    xh, xl = split(x)
    return dot(xh, tab[0]) + (dot(xl, tab[0]) + dot(xh, tab[1]))


def left_mul(tab, y):
    yh, yl = split(y)
    return dot(tab[0], yh) + (dot(tab[0], yl) + dot(tab[1], yh))


def pair(u0, u1):
    top = jnp.concatenate([u0[:, :W], u1[:, :W]], 1)
    return jnp.concatenate([top, jnp.concatenate([u0[:, W:], u1[:, W:]], 1)], 0)


def both(fields, rtab, ltab):
    out = []
    for p in range(0, len(fields), 2):
        x = jnp.concatenate([jnp.concatenate([r, i], 1) for r, i in fields[p : p + 2]], 0)
        y = right_mul(x, rtab)
        z = left_mul(ltab, pair(y[:W], y[W:]))
        out.append((z[:W, :W], z[W:, :W]))
        out.append((z[:W, W:], z[W:, W:]))
    return out


def cmul(a, b):
    return a[0] * b[0] - a[1] * b[1], a[0] * b[1] + a[1] * b[0]


def cmulc(a, b):
    return a[0] * b[0] + a[1] * b[1], a[0] * b[1] - a[1] * b[0]


def add(a, b):
    return a[0] + b[0], a[1] + b[1]


def kernel(
    off_hbm, cnt_hbm, obj, probe_hbm, meas_hbm, tab_hbm, gobj, gprobe,
    probe, meas, tab, ext0, ext1, win, tbuf, gt, gwin, pad, gext0, gext1, glow, gright, gside, gfar,
    acc, rcore, rp, zb, res, off, cnt, lsem, ssem, rsem,
):
    ty, tx = lax.axis_index("ty"), lax.axis_index("tx")
    core, y, xh = lax.rem(ty, 2), lax.rem(lax.div(ty, 2), 4), lax.div(ty, 8)
    z, x = lax.div(tx, 2), xh * 2 + lax.rem(tx, 2)

    def at(core, y, x, z):
        return {"ty": lax.div(x, 2) * 8 + y * 2 + core, "tx": z * 2 + lax.rem(x, 2)}

    ext, gext = (ext0, ext1), (gext0, gext1)
    local = []
    for src, dst in (
        (obj.at[0], ext0.at[:, 0, 0:W, :]),
        (obj.at[1], ext1.at[:, 0, 0:W, :]),
        (probe_hbm, probe),
        (tab_hbm, tab),
        (meas_hbm, meas),
        (off_hbm, off),
        (cnt_hbm, cnt),
    ):
        local.append(pltpu.make_async_copy(src, dst, lsem.at[len(local)]))
        local[-1].start()

    left, right = {"ty": ty, "tx": lax.rem(tx + 15, 16)}, {"ty": ty, "tx": lax.rem(tx + 1, 16)}
    upper, lower = {"ty": lax.rem(ty + 15, 16), "tx": tx}, {"ty": lax.rem(ty + 1, 16), "tx": tx}
    peers = [at(1 - core, y, x, z), left, right, upper, lower]
    peers += [{"ty": lax.rem(ty + 15, 16), "tx": lax.rem(tx + 15, 16)}, {"ty": lax.rem(ty + 1, 16), "tx": lax.rem(tx + 1, 16)}]
    plane = [(j, i) for j in (2, 1, 3, 0) for i in (2, 1, 3, 0)][:-1]
    in_plane = [at(core, lax.rem(y + j, 4), lax.rem(x + i, 4), z) for j, i in plane]
    in_line = [at(core, y, x, lax.rem(z + k, 8)) for k in (4, 3, 5, 2, 6, 1, 7)]
    peers += in_plane + in_line
    barrier = pltpu.get_barrier_semaphore()
    for peer in peers:
        pl.semaphore_signal(barrier, inc=1, device_id=peer, device_id_type=pl.DeviceIdType.MESH)
    pl.semaphore_wait(barrier, len(peers))

    sent = []

    def remote(src, dst, device):
        i = len(sent)
        copy = pltpu.make_async_remote_copy(
            src_ref=src, dst_ref=dst, send_sem=ssem.at[i], recv_sem=rsem.at[i],
            device_id=device, device_id_type=pl.DeviceIdType.MESH,
        )
        sent.append(copy)
        return copy

    from_right, from_lower, from_corner, far_corner = ([] for _ in range(4))
    up_left = {"ty": lax.rem(ty + 15, 16), "tx": lax.rem(tx + 15, 16)}
    for s in range(2):
        from_right.append([remote(obj.at[s, c], ext[s].at[c, 1, 0:W, :], left) for c in range(2)])
        from_lower.append(remote(obj.at[s], ext[s].at[:, 0, W : 2 * W, :], upper))
        from_corner.append([remote(ext[s].at[c, 1, 0:W, :], ext[s].at[c, 1, W : 2 * W, :], upper) for c in range(2)])
        far_corner.append([remote(obj.at[s, c], ext[s].at[c, 1, W : 2 * W, :], up_left) for c in range(2)])
    far_lower = remote(ext0.at[0, 1, W : 2 * W, :], ext0.at[0, 0, W : 2 * W, :], right)
    far_direct = remote(obj.at[0, 1], ext0.at[1, 0, W : 2 * W, :], upper)
    sends_up = jnp.logical_and(ty > 0, ty != 8)
    gets_up = jnp.logical_and(ty < 15, ty != 7)
    first = tx == 0
    sends_far, gets_far = jnp.logical_and(ty == 8, tx > 0), jnp.logical_and(ty == 7, tx < 15)
    sends_direct, gets_direct = jnp.logical_and(ty == 8, first), jnp.logical_and(ty == 7, first)
    gets_relayed = jnp.logical_and(ty == 7, tx > 0)

    def send_left(s):
        for copy in from_right[s]:
            copy.start()

    def send_up(s):
        @pl.when(jnp.logical_or(sends_up, sends_direct) if s == 0 else ty > 0)
        def _():
            from_lower[s].start()

    def relay(s):
        if s == 0:

            @pl.when(gets_far)
            def _():
                far_corner[0][0].wait_recv()
                far_lower.start()

        for c in range(2):
            from_right[s][c].wait_recv()

            @pl.when(sends_up)
            def _():
                from_corner[s][c].start()

    def send_far_up(s):
        @pl.when(sends_far)
        def _():
            for copy in (*far_corner[s], *([far_direct] if s == 0 else [])):
                copy.start()

    send_far_up(0)
    send_up(0)
    send_left(0)
    send_left(1)
    relay(0)
    send_far_up(1)
    send_up(1)

    lane = lax.broadcasted_iota(jnp.int32, (W, W), 1)

    def halo_wait(s):
        local[s].wait()

        @pl.when(jnp.logical_or(gets_up, gets_direct) if s == 0 else ty < 15)
        def _():
            from_lower[s].wait_recv()

        @pl.when(gets_up)
        def _():
            for copy in from_corner[s]:
                copy.wait_recv()

        @pl.when(gets_relayed)
        def _():
            if s == 0:
                far_lower.wait_recv()
                far_direct.wait_recv()

        @pl.when(gets_far)
        def _():
            for copy in far_corner[s][1 - s :]:
                copy.wait_recv()

    def cut(slot, s):
        oy, ox = off[0, slot], off[1, slot]
        shift = lax.rem(W - ox, W)
        parts = []
        for c in range(2):
            first = pltpu.roll(ext[s][c, 0, pl.ds(oy, W), :], shift, 1)
            second = pltpu.roll(ext[s][c, 1, pl.ds(oy, W), :], shift, 1)
            parts.append(jnp.where(lane < W - ox, first, second))
            win[s, slot, c] = parts[c]
        return tuple(parts)

    def scatter(s):
        zero = jnp.zeros((W, W), F32)
        for c in range(2):
            for slot in range(SLOTS):
                oy, ox = off[0, slot], off[1, slot]
                g = pltpu.roll(gwin[s, slot, c], ox, 1)
                for half, mask in ((0, lane >= ox), (1, lane < ox)):
                    pad[half, W : 2 * W, :] = jnp.where(mask, g, zero)
                for half in range(2):
                    v = pad[half, pl.ds(W - oy, 2 * W), :]
                    if slot == 0:
                        gext[s][c, half] = v
                    else:
                        gext[s][c, half] += v

    for part in (0, 2):
        pad[:, part * W : (part + 1) * W, :] = jnp.zeros((2, W, W), F32)
    local[2].wait()
    local[3].wait()
    local[4].wait()
    local[5].wait()
    local[6].wait()
    a_r, a_l, f_r, f_l = (tab.at[i] for i in range(4))

    halo_wait(0)

    def first_layer(slot):
        w0 = cut(slot, 0)
        ts = both([cmul((probe[m, 0], probe[m, 1]), w0) for m in range(MODES)], a_r, a_l)
        for m in range(MODES):
            tbuf[slot, m, 0], tbuf[slot, m, 1] = ts[m]

    for slot in range(0, SLOTS // 2):
        first_layer(slot)
    relay(1)
    for slot in range(SLOTS // 2, SLOTS):
        first_layer(slot)
    halo_wait(1)

    def second_layer(slot):
        w1 = cut(slot, 1)
        far = both([cmul((tbuf[slot, m, 0], tbuf[slot, m, 1]), w1) for m in range(MODES)], f_r, f_l)
        intensity = sum(r * r + i * i for r, i in far)
        live = jnp.where(slot < cnt[0, 0], 2.0, 0.0)
        d = (intensity - meas[slot]) * live
        gw = both([(r * d, i * d) for r, i in far], f_l, f_r)
        total = None
        for m in range(MODES):
            gt[slot, m, 0], gt[slot, m, 1] = cmulc(w1, gw[m])
            g = cmulc((tbuf[slot, m, 0], tbuf[slot, m, 1]), gw[m])
            total = g if total is None else add(total, g)
        gwin[1, slot, 0], gwin[1, slot, 1] = total

    for slot in range(SLOTS):
        second_layer(slot)

    to_lower = [remote(gext[s].at[:, :, W : 2 * W, :], glow.at[s], lower) for s in range(2)]
    to_right = [remote(gext[s].at[:, 1, 0:W, :], gright.at[s], right) for s in range(2)]
    side = [remote(gext[s].at[:, 1, W : 2 * W, :], gside.at[s], right) for s in range(2)]
    down_far = [remote(gext[s].at[:, 0, W : 2 * W, :], gfar.at[s], lower) for s in range(2)]

    def send_down(s):
        scatter(s)

        @pl.when(ty == 7)
        def _():
            side[s].start()

    def down(s):
        @pl.when(gets_up)
        def _():
            to_lower[s].start()

    def send_far(s):
        @pl.when(ty == 7)
        def _():
            side[s].wait_recv()
            for c in range(2):
                gext[s][c, 0, W : 2 * W, :] += gside[s, c]
            down_far[s].start()

    def send_right(s):
        @pl.when(sends_up)
        def _():
            to_lower[s].wait_recv()
            for c in range(2):
                for half in range(2):
                    gext[s][c, half, 0:W, :] += glow[s, c, half]

        to_right[s].start()

    def finish(s):
        @pl.when(ty == 8)
        def _():
            down_far[s].wait_recv()
            for c in range(2):
                gext[s][c, 0, 0:W, :] += gfar[s, c]

        to_right[s].wait_recv()
        for c in range(2):
            gobj[s, c] = gext[s][c, 0, 0:W, :] + gright[s, c]

    send_down(1)
    down(1)

    def span(start, size):
        return pl.ds(pl.multiple_of(start, size), size)

    other = at(1 - core, y, x, z)
    mine = core * W
    place = span(mine + (y * 4 + x) * 8, 8)
    by_core = [remote(acc.at[m, span((1 - core) * W, W), :], rcore.at[m], other) for m in range(MODES)]
    by_plane = []
    for g in range(2):
        spots = [span(mine + (lax.rem(y + j, 4) * 4 + lax.rem(x + i, 4)) * 8, 8) for j, i in plane]
        by_plane.append([remote(acc.at[pl.ds(2 * g, 2), spots[k], :], rp.at[g, k], in_plane[k]) for k in range(15)])
    by_line, out_plane, out_core = [], [], []
    for g in range(2):
        pair_of = pl.ds(2 * g, 2)
        by_line.append([remote(zb.at[g, z], zb.at[g, z], device) for device in in_line])
        own = res.at[pair_of, place, :]
        out_plane.append([remote(own, own, device) for device in in_plane])
        out_core.append([])
        for j in (0, 1, 3, 2):
            own = res.at[pair_of, span(mine + lax.rem(y + 4 - j, 4) * 32, 32), :]
            out_core[g].append((j, remote(own, own, other)))

    def start(copies):
        for copy in copies:
            copy.start()

    def arrive(copies):
        for copy in copies:
            copy.wait_recv()

    def scatter_core(g):
        for m in (2 * g, 2 * g + 1):
            by_core[m].wait_recv()
            acc[m, span(mine, W), :] += rcore[m]
        start(by_plane[g])

    for m in range(MODES):
        p = (probe[m, 0], probe[m, 1])
        gu = both([(gt[s, m, 0], gt[s, m, 1]) for s in range(SLOTS)], a_l, a_r)
        total = None
        for s in range(SLOTS):
            g = cmulc(p, gu[s])
            for c in range(2):
                if m == 0:
                    gwin[0, s, c] = g[c]
                else:
                    gwin[0, s, c] += g[c]
            q = cmulc((win[0, s, 0], win[0, s, 1]), gu[s])
            total = q if total is None else add(total, q)
        acc[m, 0:W, :], acc[m, W : 2 * W, :] = total
        if m % 2 == 0:
            continue
        start(by_core[m - 1 : m + 1])
        if m == MODES - 1:
            send_far(1)
            scatter_core(0)

    scatter_core(1)
    send_down(0)
    for g in range(2):
        for i in range(2):
            m = 2 * g + i
            if i == 0:
                arrive(by_plane[g])
            total = acc[m, place, :]
            for k in range(15):
                total = total + rp[g, k, i]
            zb[g, z, i] = total
        start(by_line[g])
    send_right(1)
    down(0)
    send_far(0)
    for g in range(2):
        arrive(by_line[g])
        for i in range(2):
            total = zb[g, 0, i]
            for k in range(1, 8):
                total = total + zb[g, k, i]
            res[2 * g + i, place, :] = total
        start(out_plane[g])
    send_right(0)
    for g in range(2):
        for j, copy in out_core[g]:
            arrive([out_plane[g][k] for k in range(15) if plane[k][0] == j])
            copy.start()
    finish(1)
    finish(0)
    for g in range(2):
        for _, copy in out_core[g]:
            copy.wait_recv()
        for m in (2 * g, 2 * g + 1):
            gprobe[m, 0] = res[m, 0:W, :]
            gprobe[m, 1] = res[m, W : 2 * W, :]

    groups = (
        (jnp.logical_or(sends_up, sends_direct), from_lower[:1]),
        (ty > 0, from_lower[1:]),
        (sends_up, from_corner[0] + from_corner[1]),
        (sends_far, far_corner[0] + far_corner[1] + [far_direct]),
        (gets_far, [far_lower]),
        (gets_up, to_lower),
        (ty == 7, side + down_far),
    )
    some = [id(copy) for _, copies in groups for copy in copies]
    for copy in sent:
        if id(copy) not in some:
            copy.wait_send()
    for condition, copies in groups:

        @pl.when(condition)
        def _():
            for copy in copies:
                copy.wait_send()


COPIES = 24 + MODES + 2 * 41


def on_device(object_slices, probe, measured, offsets, counts):
    vmem, hbm = (pl.BlockSpec(memory_space=s) for s in (pltpu.VMEM, pl.ANY))
    shapes = [
        (MODES, 2, W, W),
        (SLOTS, W, W),
        None,
        (2, 2, 2 * W, W),
        (2, 2, 2 * W, W),
        (2, SLOTS, 2, W, W),
        (SLOTS, MODES, 2, W, W),
        (SLOTS, MODES, 2, W, W),
        (2, SLOTS, 2, W, W),
        (2, 3 * W, W),
        (2, 2, 2 * W, W),
        (2, 2, 2 * W, W),
        (2, 2, 2, W, W),
        (2, 2, W, W),
        (2, 2, W, W),
        (2, 2, W, W),
        (MODES, 2 * W, W),
        (MODES, W, W),
        (2, 15, 2, 8, W),
        (2, 8, 2, 8, W),
        (MODES, 2 * W, W),
    ]
    scratch = [pltpu.VMEM(s, F32) if s else pltpu.VMEM((4, 2, 2 * W, 2 * W), BF16) for s in shapes]
    scratch += [pltpu.SMEM((2, SLOTS), jnp.int32), pltpu.SMEM((1, 1), jnp.int32)]
    scratch += [pltpu.SemaphoreType.DMA((7,)), pltpu.SemaphoreType.DMA((COPIES,)), pltpu.SemaphoreType.DMA((COPIES,))]
    return pl.pallas_call(
        kernel,
        out_shape=(jax.ShapeDtypeStruct((2, 2, W, W), F32), jax.ShapeDtypeStruct((MODES, 2, W, W), F32)),
        in_specs=[hbm] * 6,
        out_specs=(vmem, vmem),
        scratch_shapes=scratch,
        compiler_params=pltpu.CompilerParams(collective_id=0, has_side_effects=True),
    )(
        offsets.reshape(2, SLOTS), counts, object_slices, probe, measured.reshape(SLOTS, W, W), jnp.asarray(tables())
    )


def solution(mesh):
    in_specs = (
        P(None, None, "ty", "tx"),
        P(),
        P("ty", "tx", None, None, None),
        P(None, "ty", "tx", None),
        P("ty", "tx"),
    )
    out_specs = (P(None, None, "ty", "tx"), P())
    return jax.shard_map(
        on_device, mesh=mesh, in_specs=in_specs, out_specs=out_specs, check_vma=False
    )
```

```python
import ml_dtypes
import numpy as np

import jax
import jax.numpy as jnp
from jax import lax
from jax.experimental import pallas as pl
from jax.experimental.pallas import tpu as pltpu
from jax.sharding import PartitionSpec as P

W = 128
MODES = 4
SLOTS = 4
F32 = jnp.float32
BF16 = jnp.bfloat16


def tables():
    k = np.arange(W)
    f1 = np.exp(-2j * np.pi * (np.outer(k, k) % W) / W) / np.sqrt(W)
    freq = (k + W // 2) % W - W // 2
    h = np.exp(-2j * np.pi * (freq * freq % (4 * W)) / (4 * W))
    a = (np.conj(f1) * h[None, :]) @ f1
    out = []
    for m in (a, f1):
        right = np.block([[m.real, m.imag], [-m.imag, m.real]])
        for t in (right, right.T):
            hi = t.astype(ml_dtypes.bfloat16)
            lo = (t - hi.astype(np.float64)).astype(ml_dtypes.bfloat16)
            out.append(np.stack([hi, lo]))
    return np.stack(out)


def split(x):
    hi = x.astype(BF16)
    return hi, (x - hi.astype(F32)).astype(BF16)


def dot(a, b):
    return jnp.dot(a, b, preferred_element_type=F32)


def right_mul(x, tab):
    xh, xl = split(x)
    return dot(xh, tab[0]) + (dot(xl, tab[0]) + dot(xh, tab[1]))


def left_mul(tab, y):
    yh, yl = split(y)
    return dot(tab[0], yh) + (dot(tab[0], yl) + dot(tab[1], yh))


def pair(u0, u1):
    top = jnp.concatenate([u0[:, :W], u1[:, :W]], 1)
    return jnp.concatenate([top, jnp.concatenate([u0[:, W:], u1[:, W:]], 1)], 0)


def both(fields, rtab, ltab):
    out = []
    for p in range(0, len(fields), 2):
        x = jnp.concatenate([jnp.concatenate([r, i], 1) for r, i in fields[p : p + 2]], 0)
        y = right_mul(x, rtab)
        z = left_mul(ltab, pair(y[:W], y[W:]))
        out.append((z[:W, :W], z[W:, :W]))
        out.append((z[:W, W:], z[W:, W:]))
    return out


def cmul(a, b):
    return a[0] * b[0] - a[1] * b[1], a[0] * b[1] + a[1] * b[0]


def cmulc(a, b):
    return a[0] * b[0] + a[1] * b[1], a[0] * b[1] - a[1] * b[0]


def add(a, b):
    return a[0] + b[0], a[1] + b[1]


def kernel(
    off_hbm, cnt_hbm, obj, probe_hbm, meas_hbm, tab_hbm, gobj, gprobe,
    probe, meas, tab, ext0, ext1, win, tbuf, gt, gwin, pad, gext0, gext1, glow, gright, gside, gfar,
    acc, rcore, rp, zb, res, off, cnt, lsem, ssem, rsem,
):
    ty, tx = lax.axis_index("ty"), lax.axis_index("tx")
    core, y, xh = lax.rem(ty, 2), lax.rem(lax.div(ty, 2), 4), lax.div(ty, 8)
    z, x = lax.div(tx, 2), xh * 2 + lax.rem(tx, 2)

    def at(core, y, x, z):
        return {"ty": lax.div(x, 2) * 8 + y * 2 + core, "tx": z * 2 + lax.rem(x, 2)}

    ext, gext = (ext0, ext1), (gext0, gext1)
    local = []
    for src, dst in (
        (obj.at[0], ext0.at[:, 0, 0:W, :]),
        (obj.at[1], ext1.at[:, 0, 0:W, :]),
        (probe_hbm, probe),
        (tab_hbm, tab),
        (meas_hbm, meas),
        (off_hbm, off),
        (cnt_hbm, cnt),
    ):
        local.append(pltpu.make_async_copy(src, dst, lsem.at[len(local)]))
        local[-1].start()

    left, right = {"ty": ty, "tx": lax.rem(tx + 15, 16)}, {"ty": ty, "tx": lax.rem(tx + 1, 16)}
    upper, lower = {"ty": lax.rem(ty + 15, 16), "tx": tx}, {"ty": lax.rem(ty + 1, 16), "tx": tx}
    peers = [at(1 - core, y, x, z), left, right, upper, lower]
    peers += [{"ty": lax.rem(ty + 15, 16), "tx": lax.rem(tx + 15, 16)}, {"ty": lax.rem(ty + 1, 16), "tx": lax.rem(tx + 1, 16)}]
    plane = [(j, i) for j in (2, 1, 3, 0) for i in (2, 1, 3, 0)][:-1]
    in_plane = [at(core, lax.rem(y + j, 4), lax.rem(x + i, 4), z) for j, i in plane]
    in_line = [at(core, y, x, lax.rem(z + k, 8)) for k in (4, 3, 5, 2, 6, 1, 7)]
    peers += in_plane + in_line
    barrier = pltpu.get_barrier_semaphore()
    for peer in peers:
        pl.semaphore_signal(barrier, inc=1, device_id=peer, device_id_type=pl.DeviceIdType.MESH)
    pl.semaphore_wait(barrier, len(peers))

    sent = []

    def remote(src, dst, device):
        i = len(sent)
        copy = pltpu.make_async_remote_copy(
            src_ref=src, dst_ref=dst, send_sem=ssem.at[i], recv_sem=rsem.at[i],
            device_id=device, device_id_type=pl.DeviceIdType.MESH,
        )
        sent.append(copy)
        return copy

    from_right, from_lower, from_corner, far_corner = ([] for _ in range(4))
    up_left = {"ty": lax.rem(ty + 15, 16), "tx": lax.rem(tx + 15, 16)}
    for s in range(2):
        from_right.append([remote(obj.at[s, c], ext[s].at[c, 1, 0:W, :], left) for c in range(2)])
        from_lower.append(remote(obj.at[s], ext[s].at[:, 0, W : 2 * W, :], upper))
        from_corner.append([remote(ext[s].at[c, 1, 0:W, :], ext[s].at[c, 1, W : 2 * W, :], upper) for c in range(2)])
        far_corner.append([remote(obj.at[s, c], ext[s].at[c, 1, W : 2 * W, :], up_left) for c in range(2)])
    far_lower = remote(ext0.at[0, 1, W : 2 * W, :], ext0.at[0, 0, W : 2 * W, :], right)
    far_direct = remote(obj.at[0, 1], ext0.at[1, 0, W : 2 * W, :], upper)
    sends_up = jnp.logical_and(ty > 0, ty != 8)
    gets_up = jnp.logical_and(ty < 15, ty != 7)
    first = tx == 0
    sends_far, gets_far = jnp.logical_and(ty == 8, tx > 0), jnp.logical_and(ty == 7, tx < 15)
    sends_direct, gets_direct = jnp.logical_and(ty == 8, first), jnp.logical_and(ty == 7, first)
    gets_relayed = jnp.logical_and(ty == 7, tx > 0)

    def send_left(s):
        for copy in from_right[s]:
            copy.start()

    def send_up(s):
        @pl.when(jnp.logical_or(sends_up, sends_direct) if s == 0 else ty > 0)
        def _():
            from_lower[s].start()

    def relay(s):
        if s == 0:

            @pl.when(gets_far)
            def _():
                far_corner[0][0].wait_recv()
                far_lower.start()

        for c in range(2):
            from_right[s][c].wait_recv()

            @pl.when(sends_up)
            def _():
                from_corner[s][c].start()

    def send_far_up(s):
        @pl.when(sends_far)
        def _():
            for copy in (*far_corner[s], *([far_direct] if s == 0 else [])):
                copy.start()

    send_far_up(0)
    send_up(0)
    send_left(0)
    send_left(1)
    relay(0)
    send_far_up(1)
    send_up(1)

    lane = lax.broadcasted_iota(jnp.int32, (W, W), 1)

    def halo_wait(s):
        local[s].wait()

        @pl.when(jnp.logical_or(gets_up, gets_direct) if s == 0 else ty < 15)
        def _():
            from_lower[s].wait_recv()

        @pl.when(gets_up)
        def _():
            for copy in from_corner[s]:
                copy.wait_recv()

        @pl.when(gets_relayed)
        def _():
            if s == 0:
                far_lower.wait_recv()
                far_direct.wait_recv()

        @pl.when(gets_far)
        def _():
            for copy in far_corner[s][1 - s :]:
                copy.wait_recv()

    def cut(slot, s):
        oy, ox = off[0, slot], off[1, slot]
        shift = lax.rem(W - ox, W)
        parts = []
        for c in range(2):
            first = pltpu.roll(ext[s][c, 0, pl.ds(oy, W), :], shift, 1)
            second = pltpu.roll(ext[s][c, 1, pl.ds(oy, W), :], shift, 1)
            parts.append(jnp.where(lane < W - ox, first, second))
            win[s, slot, c] = parts[c]
        return tuple(parts)

    def scatter(s):
        zero = jnp.zeros((W, W), F32)
        for c in range(2):
            for slot in range(SLOTS):
                oy, ox = off[0, slot], off[1, slot]
                g = pltpu.roll(gwin[s, slot, c], ox, 1)
                for half, mask in ((0, lane >= ox), (1, lane < ox)):
                    pad[half, W : 2 * W, :] = jnp.where(mask, g, zero)
                for half in range(2):
                    v = pad[half, pl.ds(W - oy, 2 * W), :]
                    if slot == 0:
                        gext[s][c, half] = v
                    else:
                        gext[s][c, half] += v

    for part in (0, 2):
        pad[:, part * W : (part + 1) * W, :] = jnp.zeros((2, W, W), F32)
    local[2].wait()
    local[3].wait()
    local[4].wait()
    local[5].wait()
    local[6].wait()
    a_r, a_l, f_r, f_l = (tab.at[i] for i in range(4))

    halo_wait(0)

    def first_layer(slot):
        w0 = cut(slot, 0)
        ts = both([cmul((probe[m, 0], probe[m, 1]), w0) for m in range(MODES)], a_r, a_l)
        for m in range(MODES):
            tbuf[slot, m, 0], tbuf[slot, m, 1] = ts[m]

    for slot in range(0, SLOTS // 2):
        first_layer(slot)
    relay(1)
    for slot in range(SLOTS // 2, SLOTS):
        first_layer(slot)
    halo_wait(1)

    def second_layer(slot):
        w1 = cut(slot, 1)
        far = both([cmul((tbuf[slot, m, 0], tbuf[slot, m, 1]), w1) for m in range(MODES)], f_r, f_l)
        intensity = sum(r * r + i * i for r, i in far)
        live = jnp.where(slot < cnt[0, 0], 2.0, 0.0)
        d = (intensity - meas[slot]) * live
        gw = both([(r * d, i * d) for r, i in far], f_l, f_r)
        total = None
        for m in range(MODES):
            gt[slot, m, 0], gt[slot, m, 1] = cmulc(w1, gw[m])
            g = cmulc((tbuf[slot, m, 0], tbuf[slot, m, 1]), gw[m])
            total = g if total is None else add(total, g)
        gwin[1, slot, 0], gwin[1, slot, 1] = total

    for slot in range(SLOTS):
        second_layer(slot)

    to_lower = [remote(gext[s].at[:, :, W : 2 * W, :], glow.at[s], lower) for s in range(2)]
    to_right = [remote(gext[s].at[:, 1, 0:W, :], gright.at[s], right) for s in range(2)]
    side = [remote(gext[s].at[:, 1, W : 2 * W, :], gside.at[s], right) for s in range(2)]
    down_far = [remote(gext[s].at[:, 0, W : 2 * W, :], gfar.at[s], lower) for s in range(2)]

    def send_down(s):
        scatter(s)

        @pl.when(ty == 7)
        def _():
            side[s].start()

    def down(s):
        @pl.when(gets_up)
        def _():
            to_lower[s].start()

    def send_far(s):
        @pl.when(ty == 7)
        def _():
            side[s].wait_recv()
            for c in range(2):
                gext[s][c, 0, W : 2 * W, :] += gside[s, c]
            down_far[s].start()

    def send_right(s):
        @pl.when(sends_up)
        def _():
            to_lower[s].wait_recv()
            for c in range(2):
                for half in range(2):
                    gext[s][c, half, 0:W, :] += glow[s, c, half]

        to_right[s].start()

    def finish(s):
        @pl.when(ty == 8)
        def _():
            down_far[s].wait_recv()
            for c in range(2):
                gext[s][c, 0, 0:W, :] += gfar[s, c]

        to_right[s].wait_recv()
        for c in range(2):
            gobj[s, c] = gext[s][c, 0, 0:W, :] + gright[s, c]

    send_down(1)
    down(1)

    def span(start, size):
        return pl.ds(pl.multiple_of(start, size), size)

    other = at(1 - core, y, x, z)
    mine = core * W
    place = span(mine + (y * 4 + x) * 8, 8)
    by_core = [remote(acc.at[m, span((1 - core) * W, W), :], rcore.at[m], other) for m in range(MODES)]
    by_plane = []
    for g in range(2):
        spots = [span(mine + (lax.rem(y + j, 4) * 4 + lax.rem(x + i, 4)) * 8, 8) for j, i in plane]
        by_plane.append([remote(acc.at[pl.ds(2 * g, 2), spots[k], :], rp.at[g, k], in_plane[k]) for k in range(15)])
    by_line, out_plane, out_core = [], [], []
    for g in range(2):
        pair_of = pl.ds(2 * g, 2)
        by_line.append([remote(zb.at[g, z], zb.at[g, z], device) for device in in_line])
        own = res.at[pair_of, place, :]
        out_plane.append([remote(own, own, device) for device in in_plane])
        out_core.append([])
        for j in (0, 1, 3, 2):
            own = res.at[pair_of, span(mine + lax.rem(y + 4 - j, 4) * 32, 32), :]
            out_core[g].append((j, remote(own, own, other)))

    def start(copies):
        for copy in copies:
            copy.start()

    def arrive(copies):
        for copy in copies:
            copy.wait_recv()

    def scatter_core(g):
        for m in (2 * g, 2 * g + 1):
            by_core[m].wait_recv()
            acc[m, span(mine, W), :] += rcore[m]
        start(by_plane[g])

    for m in range(MODES):
        p = (probe[m, 0], probe[m, 1])
        gu = both([(gt[s, m, 0], gt[s, m, 1]) for s in range(SLOTS)], a_l, a_r)
        total = None
        for s in range(SLOTS):
            g = cmulc(p, gu[s])
            for c in range(2):
                if m == 0:
                    gwin[0, s, c] = g[c]
                else:
                    gwin[0, s, c] += g[c]
            q = cmulc((win[0, s, 0], win[0, s, 1]), gu[s])
            total = q if total is None else add(total, q)
        acc[m, 0:W, :], acc[m, W : 2 * W, :] = total
        if m == MODES - 2:
            scatter_core(0)
        if m % 2 == 0:
            continue
        start(by_core[m - 1 : m + 1])
        if m == MODES - 1:
            send_far(1)

    scatter_core(1)
    send_down(0)
    for g in range(2):
        for i in range(2):
            m = 2 * g + i
            if i == 0:
                arrive(by_plane[g])
            total = acc[m, place, :]
            for k in range(15):
                total = total + rp[g, k, i]
            zb[g, z, i] = total
        start(by_line[g])
    send_right(1)
    down(0)
    send_far(0)
    for g in range(2):
        arrive(by_line[g])
        for i in range(2):
            total = zb[g, 0, i]
            for k in range(1, 8):
                total = total + zb[g, k, i]
            res[2 * g + i, place, :] = total
        start(out_plane[g])
    send_right(0)
    for g in range(2):
        for j, copy in out_core[g]:
            arrive([out_plane[g][k] for k in range(15) if plane[k][0] == j])
            copy.start()
    finish(1)
    finish(0)
    for g in range(2):
        for _, copy in out_core[g]:
            copy.wait_recv()
        for m in (2 * g, 2 * g + 1):
            gprobe[m, 0] = res[m, 0:W, :]
            gprobe[m, 1] = res[m, W : 2 * W, :]

    groups = (
        (jnp.logical_or(sends_up, sends_direct), from_lower[:1]),
        (ty > 0, from_lower[1:]),
        (sends_up, from_corner[0] + from_corner[1]),
        (sends_far, far_corner[0] + far_corner[1] + [far_direct]),
        (gets_far, [far_lower]),
        (gets_up, to_lower),
        (ty == 7, side + down_far),
    )
    some = [id(copy) for _, copies in groups for copy in copies]
    for copy in sent:
        if id(copy) not in some:
            copy.wait_send()
    for condition, copies in groups:

        @pl.when(condition)
        def _():
            for copy in copies:
                copy.wait_send()


def hand_over(gobj, gprobe, gobj_out, gprobe_out, gobj_held, gprobe_held, in_sem, out_sem):
    parts = [(gobj, gobj_held, gobj_out, i) for i in range(2)]
    parts += [(gprobe, gprobe_held, gprobe_out, i) for i in range(MODES)]
    taken = [pltpu.make_async_copy(a.at[i], b.at[i], in_sem.at[k]) for k, (a, b, _, i) in enumerate(parts)]
    given = [pltpu.make_async_copy(b.at[i], c.at[i], out_sem.at[k]) for k, (_, b, c, i) in enumerate(parts)]
    for copy in taken:
        copy.start()
    for first, second in zip(taken, given, strict=True):
        first.wait()
        second.start()
    for copy in given:
        copy.wait()


COPIES = 24 + MODES + 2 * 41


def on_device(object_slices, probe, measured, offsets, counts):
    vmem, hbm = (pl.BlockSpec(memory_space=s) for s in (pltpu.VMEM, pl.ANY))
    shapes = [
        (MODES, 2, W, W),
        (SLOTS, W, W),
        None,
        (2, 2, 2 * W, W),
        (2, 2, 2 * W, W),
        (2, SLOTS, 2, W, W),
        (SLOTS, MODES, 2, W, W),
        (SLOTS, MODES, 2, W, W),
        (2, SLOTS, 2, W, W),
        (2, 3 * W, W),
        (2, 2, 2 * W, W),
        (2, 2, 2 * W, W),
        (2, 2, 2, W, W),
        (2, 2, W, W),
        (2, 2, W, W),
        (2, 2, W, W),
        (MODES, 2 * W, W),
        (MODES, W, W),
        (2, 15, 2, 8, W),
        (2, 8, 2, 8, W),
        (MODES, 2 * W, W),
    ]
    scratch = [pltpu.VMEM(s, F32) if s else pltpu.VMEM((4, 2, 2 * W, 2 * W), BF16) for s in shapes]
    scratch += [pltpu.SMEM((2, SLOTS), jnp.int32), pltpu.SMEM((1, 1), jnp.int32)]
    scratch += [pltpu.SemaphoreType.DMA((7,)), pltpu.SemaphoreType.DMA((COPIES,)), pltpu.SemaphoreType.DMA((COPIES,))]
    grads = pl.pallas_call(
        kernel,
        out_shape=(jax.ShapeDtypeStruct((2, 2, W, W), F32), jax.ShapeDtypeStruct((MODES, 2, W, W), F32)),
        in_specs=[hbm] * 6,
        out_specs=(vmem, vmem),
        scratch_shapes=scratch,
        compiler_params=pltpu.CompilerParams(collective_id=0, has_side_effects=True),
    )(
        offsets.reshape(2, SLOTS), counts, object_slices, probe, measured.reshape(SLOTS, W, W), jnp.asarray(tables())
    )
    pieces = 2 + MODES
    return pl.pallas_call(
        hand_over,
        out_shape=tuple(jax.ShapeDtypeStruct(g.shape, F32) for g in grads),
        in_specs=[hbm, hbm],
        out_specs=(hbm, hbm),
        scratch_shapes=[
            pltpu.VMEM(grads[0].shape, F32),
            pltpu.VMEM(grads[1].shape, F32),
            pltpu.SemaphoreType.DMA((pieces,)),
            pltpu.SemaphoreType.DMA((pieces,)),
        ],
    )(*grads)


def solution(mesh):
    in_specs = (
        P(None, None, "ty", "tx"),
        P(),
        P("ty", "tx", None, None, None),
        P(None, "ty", "tx", None),
        P("ty", "tx"),
    )
    out_specs = (P(None, None, "ty", "tx"), P())
    return jax.shard_map(
        on_device, mesh=mesh, in_specs=in_specs, out_specs=out_specs, check_vma=False
    )
```
